256 devices in a mesh: rows: 32 (over x, z), vecs: 8 (over y, core).
Axes of the slice: x: 4, y: 4, z: 8, core: 2. Of those that a mesh axis runs over, the one named last changes fastest.
Arguments:
- coords: float32 [3, 8192], P(None, ('rows', 'vecs')), may hold values from 0 to 1
- old_vectors: bfloat16 [8192, 16384], P('rows', 'vecs'), may hold values from -0.078125 to 0.078125
- pivots: int32 [2, 128], replicated, may hold values from 0 to 8191, as said below
- slots: int32 [8192], replicated, may hold values from 0 to 8191, each once
Outputs:
- new_vectors: float32 [8192, 256], P(('rows', 'vecs'))
The draws below stay inside these ranges and needn't reach their ends.
Inputs may be any that keep to these rules, and one draw needn't show every extreme that they name: `pivots`: all 256 pivot numbers are distinct. `slots`: each window row belongs to exactly one point.
All inputs are finite; a program needn't handle non-finite values.
Results may differ from the reference program's by a relative error of at most 0.0003.
Values may be sent and summed in bfloat16 or wider, within the bound.
A program may use at most 64 MiB of HBM per device.

```python
import jax
import jax.numpy as jnp
from jax import lax

VECTORS = 16384
B = 128
PANELS = 2
WINDOW = 8192


def draw_old_vectors(key, part):
    spread = (6.0 / VECTORS) ** 0.5
    values = jnp.clip(jax.random.normal(key, (WINDOW, VECTORS), jnp.float32) * spread, -4.0 * spread, 4.0 * spread)
    return values.astype(jnp.bfloat16)


def draw_pivots(key, part):
    shuffled = jax.random.permutation(jax.random.fold_in(key, 7), WINDOW)
    return shuffled[:PANELS * B].reshape(PANELS, B).astype(jnp.int32)


def levels(own_key, dims, shards, smallest, high):
    gain = 1.0
    for axis_at, parts in shards:
        steps = jax.random.uniform(jax.random.fold_in(jax.random.fold_in(own_key, 6), axis_at), (parts,), jnp.float32, smallest / len(shards), high / len(shards))
        gain = gain * jnp.repeat(jnp.exp(steps), dims[axis_at] // parts).reshape((-1,) + (1,) * (len(dims) - 1 - axis_at))
    return gain


def setup_inputs(seed: int = 0) -> dict:
    splits = jax.random.split(jax.random.key(seed), 5)
    return {
        "coords": jnp.clip(1.0 * jax.random.uniform(splits[0], (3, WINDOW), jnp.float32) ** levels(splits[0], (3, WINDOW), ((1, 256),), -0.2, 0.2), 0.0, 1.0),
        "old_vectors": draw_old_vectors(jax.random.fold_in(splits[4], 71), 0),
        "pivots": draw_pivots(jax.random.fold_in(splits[4], 71), 0),
        "slots": jax.random.permutation(splits[3], WINDOW).astype(jnp.int32),
    }


length_scale = 0.5
noise_shift = 12.0

def matern(points, centers):
    dist_sq = jnp.zeros((points.shape[1], centers.shape[1]), jnp.float32)
    for component in range(3):
        differ = points[component][:, None] - centers[component][None, :]
        dist_sq = dist_sq + differ * differ
    scaled = jnp.sqrt(5.0 * dist_sq) / length_scale
    return (1.0 + scaled + scaled * scaled / 3.0) * jnp.exp(-scaled)

def reference(coords, old_vectors, pivots, slots):
    wanted = jnp.take(slots, pivots, axis=0).astype(jnp.int32)
    positions = jnp.arange(WINDOW, dtype=jnp.int32)
    new_panels = []
    for panel in range(PANELS):
        chosen = wanted[panel]
        centers = jnp.take(coords, chosen, axis=1)
        kernel = matern(coords, centers) + noise_shift * (positions[:, None] == chosen[None, :]).astype(jnp.float32)
        old_pivot = jnp.take(old_vectors, chosen, axis=0)
        current = kernel - jnp.dot(old_vectors.astype(jnp.float32), old_pivot.T.astype(jnp.float32), preferred_element_type=jnp.float32)
        if new_panels:
            stacked = jnp.concatenate(new_panels, axis=1)
            earlier = jnp.take(stacked, chosen, axis=0)
            current = current - jnp.dot(stacked.astype(jnp.float32), earlier.T.astype(jnp.float32), precision=lax.Precision.HIGHEST, preferred_element_type=jnp.float32)
        block = jnp.take(current, chosen, axis=0)
        factor = jnp.linalg.cholesky(block)
        fresh = jax.scipy.linalg.solve_triangular(factor, current.T, lower=True).T
        new_panels.append(fresh)
    return jnp.concatenate(new_panels, axis=1)
```

```python
import functools

import jax
import jax.numpy as jnp
from jax import lax
from jax.experimental import pallas as pl
from jax.experimental.pallas import tpu as pltpu
from jax.sharding import PartitionSpec as P

length_scale = 0.5
noise_shift = 12.0
MESH = pl.DeviceIdType.MESH

X = 4
Z = 8
V = 8
PIV = 256
HIGHEST = lax.Precision.HIGHEST


def matern(points, centers):
    dist_sq = jnp.zeros((points.shape[1], centers.shape[1]), jnp.float32)
    for component in range(3):
        differ = points[component][:, None] - centers[component][None, :]
        dist_sq = dist_sq + differ * differ
    scaled = jnp.sqrt(5.0 * dist_sq) / length_scale
    return (1.0 + scaled + scaled * scaled / 3.0) * jnp.exp(-scaled)


def dot_t(a, b):
    return lax.dot_general(a, b, (((1,), (1,)), ((), ())), preferred_element_type=jnp.float32)


def exchange(
    masked, old, spots, block_out, rows_out, spots_out,
    in_x, sum_x, in_z, cols, piv, sx, sz, sv, part_c, part_a, in_c, in_a,
    x_send, x_recv, z_send, z_recv, v_send, v_recv,
):
    row = lax.axis_index("rows")
    vec = lax.axis_index("vecs")
    x = row // Z
    z = row % Z
    chunk = PIV // X
    width = old.shape[1] // Z
    share = PIV // V

    def x_peer(k):
        return lax.rem(x + k, X)

    def z_peer(k):
        return lax.rem(z + k, Z)

    def v_peer(k):
        return lax.rem(vec + k, V)

    barrier = pltpu.get_barrier_semaphore()
    for k in range(1, X):
        pl.semaphore_signal(barrier, inc=1, device_id={"rows": x_peer(k) * Z + z, "vecs": vec}, device_id_type=MESH)
    for k in range(1, Z):
        pl.semaphore_signal(barrier, inc=1, device_id={"rows": x * Z + z_peer(k), "vecs": vec}, device_id_type=MESH)
    for k in range(1, V):
        pl.semaphore_signal(barrier, inc=1, device_id={"rows": row, "vecs": v_peer(k)}, device_id_type=MESH)
    pl.semaphore_wait(barrier, X + Z + V - 3)

    def to_x(k, src, dst, stage):
        return pltpu.make_async_remote_copy(
            src_ref=src, dst_ref=dst, send_sem=x_send.at[stage, k - 1], recv_sem=x_recv.at[stage, k - 1],
            device_id={"rows": x_peer(k) * Z + z, "vecs": vec}, device_id_type=MESH)

    def to_z(k, src, dst, stage):
        return pltpu.make_async_remote_copy(
            src_ref=src, dst_ref=dst, send_sem=z_send.at[stage, k - 1], recv_sem=z_recv.at[stage, k - 1],
            device_id={"rows": x * Z + z_peer(k), "vecs": vec}, device_id_type=MESH)

    def to_v(k, src, dst, stage):
        return pltpu.make_async_remote_copy(
            src_ref=src, dst_ref=dst, send_sem=v_send.at[stage, k - 1], recv_sem=v_recv.at[stage, k - 1],
            device_id={"rows": row, "vecs": v_peer(k)}, device_id_type=MESH)

    def start(copies):
        for copy in copies:
            copy.start()

    def wait(copies):
        for copy in copies:
            copy.wait()

    copies = [to_x(k, masked.at[pl.ds(x_peer(k) * chunk, chunk), :], in_x.at[k - 1], 0) for k in range(1, X)]
    copies += [to_x(k, spots, sx.at[k - 1], 1) for k in range(1, X)]
    start(copies)
    wait(copies)
    sum_x[...] = masked[pl.ds(x * chunk, chunk), :] + in_x[0] + in_x[1] + in_x[2]
    spots_x = spots[...] + sx[0] + sx[1] + sx[2]
    sx[0] = spots_x

    def columns(at):
        return pl.ds(pl.multiple_of(at * width, width), width)

    copies = [to_z(k, sum_x.at[:, columns(z_peer(k))], in_z.at[k - 1], 0) for k in range(1, Z)]
    copies += [to_z(k, sx.at[0], sz.at[k - 1], 1) for k in range(1, Z)]
    start(copies)
    wait(copies)
    total = sum_x[:, columns(z)]
    spots_z = sx[0]
    for k in range(Z - 1):
        total = total + in_z[k]
        spots_z = spots_z + sz[k]
    cols[:, columns(z)] = total
    sz[0] = spots_z

    copies = [to_z(k, cols.at[:, columns(z)], cols.at[:, columns(z)], 2) for k in range(1, Z)]
    start(copies)
    wait(copies)
    mine = pl.ds(x * chunk, chunk)
    piv[mine, :] = cols[...]
    copies = [to_x(k, cols, piv.at[mine, :], 2) for k in range(1, X)]
    start(copies)
    wait(copies)

    pivots = piv[...]
    part_a[...] = dot_t(pivots, pivots)
    part_c[...] = dot_t(old[...], pivots)

    def rows(at):
        return pl.ds(at * share, share)

    copies_a = [to_v(k, part_a.at[rows(v_peer(k)), :], in_a.at[k - 1], 0) for k in range(1, V)]
    copies_a += [to_v(k, sz.at[0], sv.at[k - 1], 3) for k in range(1, V)]
    copies_c = [to_v(k, part_c.at[rows(v_peer(k)), :], in_c.at[k - 1], 1) for k in range(1, V)]
    start(copies_a)
    start(copies_c)
    wait(copies_a)
    total = part_a[rows(vec), :]
    spots_v = sz[0]
    for k in range(V - 1):
        total = total + in_a[k]
        spots_v = spots_v + sv[k]
    block_out[rows(vec), :] = total
    spots_out[...] = spots_v
    copies = [to_v(k, block_out.at[rows(vec), :], block_out.at[rows(vec), :], 2) for k in range(1, V)]
    start(copies)
    wait(copies_c)
    total = part_c[rows(vec), :]
    for k in range(V - 1):
        total = total + in_c[k]
    rows_out[...] = total
    wait(copies)


def shards(coords, old_vectors, pivots, slots):
    row_block, depth = old_vectors.shape
    share = coords.shape[1]
    block_first = lax.axis_index("rows") * row_block
    share_first = block_first + lax.axis_index("vecs") * share
    wanted = jnp.take(slots, pivots.reshape(-1), axis=0)
    hot = (wanted[:, None] - block_first == jnp.arange(row_block, dtype=jnp.int32)[None, :]).astype(jnp.bfloat16)
    masked = jnp.dot(hot, old_vectors, preferred_element_type=jnp.float32).astype(jnp.bfloat16)
    hot_share = (jnp.arange(share, dtype=jnp.int32)[:, None] == wanted[None, :] - share_first).astype(jnp.float32)
    spots = jnp.sum(coords[:, :, None] * hot_share[None, :, :], axis=1)
    spots = jnp.concatenate([spots, jnp.zeros((5, PIV), jnp.float32)], axis=0)

    vmem = pl.BlockSpec(memory_space=pltpu.VMEM)
    f32 = jnp.float32
    bf16 = jnp.bfloat16
    block, rows, spots = pl.pallas_call(
        exchange,
        out_shape=(
            jax.ShapeDtypeStruct((PIV, PIV), f32),
            jax.ShapeDtypeStruct((share, PIV), f32),
            jax.ShapeDtypeStruct((8, PIV), f32),
        ),
        in_specs=[vmem] * 3,
        out_specs=(vmem,) * 3,
        scratch_shapes=[
            pltpu.VMEM((X - 1, PIV // X, depth), bf16),
            pltpu.VMEM((PIV // X, depth), bf16),
            pltpu.VMEM((Z - 1, PIV // X, depth // Z), bf16),
            pltpu.VMEM((PIV // X, depth), bf16),
            pltpu.VMEM((PIV, depth), bf16),
            pltpu.VMEM((X - 1, 8, PIV), f32),
            pltpu.VMEM((Z - 1, 8, PIV), f32),
            pltpu.VMEM((V - 1, 8, PIV), f32),
            pltpu.VMEM((row_block, PIV), f32),
            pltpu.VMEM((PIV, PIV), f32),
            pltpu.VMEM((V - 1, share, PIV), f32),
            pltpu.VMEM((V - 1, PIV // V, PIV), f32),
            pltpu.SemaphoreType.DMA((3, X - 1)),
            pltpu.SemaphoreType.DMA((3, X - 1)),
            pltpu.SemaphoreType.DMA((3, Z - 1)),
            pltpu.SemaphoreType.DMA((3, Z - 1)),
            pltpu.SemaphoreType.DMA((4, V - 1)),
            pltpu.SemaphoreType.DMA((4, V - 1)),
        ],
        compiler_params=pltpu.CompilerParams(collective_id=0, has_side_effects=True),
    )(masked, old_vectors, spots)

    centers = spots[:3]
    my_rows = share_first + jnp.arange(share, dtype=jnp.int32)
    diagonal = noise_shift * jnp.eye(PIV, dtype=f32)
    block = matern(centers, centers) + diagonal - block
    current = matern(coords, centers) + noise_shift * (my_rows[:, None] == wanted[None, :]).astype(f32) - rows
    factor = jnp.linalg.cholesky(block, symmetrize_input=False)
    return jax.scipy.linalg.solve_triangular(factor, current.T, lower=True).T


def solution(mesh):
    in_specs = (P(None, ("rows", "vecs")), P("rows", "vecs"), P(), P())
    out_specs = P(("rows", "vecs"), None)
    return jax.shard_map(shards, mesh=mesh, in_specs=in_specs, out_specs=out_specs, check_vma=False)
```

```python
import functools

import jax
import jax.numpy as jnp
from jax import lax
from jax.experimental import pallas as pl
from jax.experimental.pallas import tpu as pltpu
from jax.sharding import PartitionSpec as P

length_scale = 0.5
noise_shift = 12.0
MESH = pl.DeviceIdType.MESH

X = 4
Z = 8
V = 8
PIV = 256
G = 8
LANES = 128


def column_of(row, length):
    eye = lax.broadcasted_iota(jnp.int32, (length, length), 0) == lax.broadcasted_iota(jnp.int32, (length, length), 1)
    return jnp.sum(jnp.where(eye, row, 0.0), axis=1, keepdims=True)


def kernel_value(points, centers):
    dist_sq = None
    for a, b in zip(points, centers):
        differ = a - b
        dist_sq = differ * differ if dist_sq is None else dist_sq + differ * differ
    scaled = jnp.sqrt(5.0 * dist_sq) * 2.0
    return (1.0 + scaled + scaled * scaled * (1.0 / 3.0)) * jnp.exp(-scaled)


def finish(block, rows, spots, coords, place, out, mat):
    share = rows.shape[0]
    tiles = PIV // LANES
    centers = [spots[c : c + 1, :] for c in range(3)]
    for t in range(tiles):
        lanes = slice(t * LANES, (t + 1) * LANES)
        points = [column_of(spots[c : c + 1, lanes], LANES) for c in range(3)]
        value = kernel_value(points, centers)
        at = lax.broadcasted_iota(jnp.int32, (LANES, PIV), 0) + t * LANES
        value = value + jnp.where(at == lax.broadcasted_iota(jnp.int32, (LANES, PIV), 1), 12.0, 0.0)
        mat[lanes, :] = value - block[lanes, :]
    points = [column_of(coords[c : c + 1, :], share) for c in range(3)]
    value = kernel_value(points, centers)
    at = lax.broadcasted_iota(jnp.int32, (share, PIV), 0)
    value = value + jnp.where(at == place[...], 12.0, 0.0)
    mat[PIV : PIV + share, :] = value - rows[...]

    lane = lax.broadcasted_iota(jnp.int32, (G, LANES), 1)
    full = (G, LANES)
    groups_all = (PIV + share) // G
    for k in range(PIV // G):
        first = k * G
        tile = first // LANES
        off = first % LANES
        own = slice(first, first + G)
        home = slice(tile * LANES, (tile + 1) * LANES)
        diag = mat[own, home]
        col = [jnp.broadcast_to(diag[:, off + m : off + m + 1], full) for m in range(G)]
        s = [[None] * G for _ in range(G)]
        for m in range(G):
            for i in range(m, G):
                s[i][m] = jnp.broadcast_to(col[m][i : i + 1, :], full)
        inv = [None] * G
        for m in range(G):
            inv[m] = lax.rsqrt(s[m][m])
            for i in range(m + 1, G):
                s[i][m] = s[i][m] * inv[m]
            for n in range(m + 1, G):
                for i in range(n, G):
                    s[i][n] = s[i][n] - s[i][m] * s[n][m]
        live = range(tile, tiles)
        u = {}
        w = {}
        for t in live:
            lanes = slice(t * LANES, (t + 1) * LANES)
            part = mat[own, lanes]
            us = []
            for i in range(G):
                value = jnp.broadcast_to(part[i : i + 1, :], full)
                for m in range(i):
                    value = value - s[i][m] * us[m]
                us.append(value * inv[i])
            ws = [None] * G
            for i in reversed(range(G)):
                value = us[i]
                for m in range(i + 1, G):
                    value = value - s[m][i] * ws[m]
                ws[i] = value * inv[i]
            u[t], w[t] = us, ws
        for g in range(k + 1, groups_all):
            at = slice(g * G, (g + 1) * G)
            source = mat[at, home]
            cols = [jnp.broadcast_to(source[:, off + m : off + m + 1], full) for m in range(G)]
            if g < PIV // G:
                for t in live:
                    lanes = slice(t * LANES, (t + 1) * LANES)
                    value = source if t == tile else mat[at, lanes]
                    acc = cols[0] * w[t][0]
                    for m in range(1, G):
                        acc = acc + cols[m] * w[t][m]
                    mat[at, lanes] = value - acc
            else:
                made = []
                for i in range(G):
                    value = cols[i]
                    for m in range(i):
                        value = value - s[i][m] * made[m]
                    made.append(value * inv[i])
                for t in live:
                    lanes = slice(t * LANES, (t + 1) * LANES)
                    value = source if t == tile else mat[at, lanes]
                    acc = made[0] * u[t][0]
                    for m in range(1, G):
                        acc = acc + made[m] * u[t][m]
                    value = value - acc
                    if t == tile:
                        for i in range(G):
                            value = jnp.where(lane == off + i, made[i], value)
                    mat[at, lanes] = value
    out[...] = mat[PIV : PIV + share, :]


def dot_t(a, b):
    return lax.dot_general(a, b, (((1,), (1,)), ((), ())), preferred_element_type=jnp.float32)


def exchange(
    masked, old, spots, block_out, rows_out, spots_out,
    in_x, sum_x, in_z, cols, piv, sx, sz, sv, part_c, part_a, in_c, in_a,
    x_send, x_recv, z_send, z_recv, v_send, v_recv,
):
    row = lax.axis_index("rows")
    vec = lax.axis_index("vecs")
    x = row // Z
    z = row % Z
    chunk = PIV // X
    width = old.shape[1] // Z
    share = PIV // V

    def x_peer(k):
        return lax.rem(x + k, X)

    def z_peer(k):
        return lax.rem(z + k, Z)

    def v_peer(k):
        return lax.rem(vec + k, V)

    barrier = pltpu.get_barrier_semaphore()
    for k in range(1, X):
        pl.semaphore_signal(barrier, inc=1, device_id={"rows": x_peer(k) * Z + z, "vecs": vec}, device_id_type=MESH)
    for k in range(1, Z):
        pl.semaphore_signal(barrier, inc=1, device_id={"rows": x * Z + z_peer(k), "vecs": vec}, device_id_type=MESH)
    for k in range(1, V):
        pl.semaphore_signal(barrier, inc=1, device_id={"rows": row, "vecs": v_peer(k)}, device_id_type=MESH)
    pl.semaphore_wait(barrier, X + Z + V - 3)

    def to_x(k, src, dst, stage):
        return pltpu.make_async_remote_copy(
            src_ref=src, dst_ref=dst, send_sem=x_send.at[stage, k - 1], recv_sem=x_recv.at[stage, k - 1],
            device_id={"rows": x_peer(k) * Z + z, "vecs": vec}, device_id_type=MESH)

    def to_z(k, src, dst, stage):
        return pltpu.make_async_remote_copy(
            src_ref=src, dst_ref=dst, send_sem=z_send.at[stage, k - 1], recv_sem=z_recv.at[stage, k - 1],
            device_id={"rows": x * Z + z_peer(k), "vecs": vec}, device_id_type=MESH)

    def to_v(k, src, dst, stage):
        return pltpu.make_async_remote_copy(
            src_ref=src, dst_ref=dst, send_sem=v_send.at[stage, k - 1], recv_sem=v_recv.at[stage, k - 1],
            device_id={"rows": row, "vecs": v_peer(k)}, device_id_type=MESH)

    def start(copies):
        for copy in copies:
            copy.start()

    def wait(copies):
        for copy in copies:
            copy.wait()

    copies = [to_x(k, masked.at[pl.ds(x_peer(k) * chunk, chunk), :], in_x.at[k - 1], 0) for k in range(1, X)]
    copies += [to_x(k, spots, sx.at[k - 1], 1) for k in range(1, X)]
    start(copies)
    wait(copies)
    sum_x[...] = masked[pl.ds(x * chunk, chunk), :] + in_x[0] + in_x[1] + in_x[2]
    spots_x = spots[...] + sx[0] + sx[1] + sx[2]
    sx[0] = spots_x

    def columns(at):
        return pl.ds(pl.multiple_of(at * width, width), width)

    copies = [to_z(k, sum_x.at[:, columns(z_peer(k))], in_z.at[k - 1], 0) for k in range(1, Z)]
    copies += [to_z(k, sx.at[0], sz.at[k - 1], 1) for k in range(1, Z)]
    start(copies)
    wait(copies)
    total = sum_x[:, columns(z)]
    spots_z = sx[0]
    for k in range(Z - 1):
        total = total + in_z[k]
        spots_z = spots_z + sz[k]
    cols[:, columns(z)] = total
    sz[0] = spots_z

    copies = [to_z(k, cols.at[:, columns(z)], cols.at[:, columns(z)], 2) for k in range(1, Z)]
    start(copies)
    wait(copies)
    mine = pl.ds(x * chunk, chunk)
    piv[mine, :] = cols[...]
    copies = [to_x(k, cols, piv.at[mine, :], 2) for k in range(1, X)]
    start(copies)
    wait(copies)

    pivots = piv[...]
    part_a[...] = dot_t(pivots, pivots)
    part_c[...] = dot_t(old[...], pivots)

    def rows(at):
        return pl.ds(at * share, share)

    copies_a = [to_v(k, part_a.at[rows(v_peer(k)), :], in_a.at[k - 1], 0) for k in range(1, V)]
    copies_a += [to_v(k, sz.at[0], sv.at[k - 1], 3) for k in range(1, V)]
    copies_c = [to_v(k, part_c.at[rows(v_peer(k)), :], in_c.at[k - 1], 1) for k in range(1, V)]
    start(copies_a)
    start(copies_c)
    wait(copies_a)
    total = part_a[rows(vec), :]
    spots_v = sz[0]
    for k in range(V - 1):
        total = total + in_a[k]
        spots_v = spots_v + sv[k]
    block_out[rows(vec), :] = total
    spots_out[...] = spots_v
    copies = [to_v(k, block_out.at[rows(vec), :], block_out.at[rows(vec), :], 2) for k in range(1, V)]
    start(copies)
    wait(copies_c)
    total = part_c[rows(vec), :]
    for k in range(V - 1):
        total = total + in_c[k]
    rows_out[...] = total
    wait(copies)


def shards(coords, old_vectors, pivots, slots):
    row_block, depth = old_vectors.shape
    share = coords.shape[1]
    block_first = lax.axis_index("rows") * row_block
    share_first = block_first + lax.axis_index("vecs") * share
    wanted = jnp.take(slots, pivots.reshape(-1), axis=0)
    hot = (wanted[:, None] - block_first == jnp.arange(row_block, dtype=jnp.int32)[None, :]).astype(jnp.bfloat16)
    masked = jnp.dot(hot, old_vectors, preferred_element_type=jnp.float32).astype(jnp.bfloat16)
    hot_share = (jnp.arange(share, dtype=jnp.int32)[:, None] == wanted[None, :] - share_first).astype(jnp.float32)
    spots = jnp.sum(coords[:, :, None] * hot_share[None, :, :], axis=1)
    spots = jnp.concatenate([spots, jnp.zeros((5, PIV), jnp.float32)], axis=0)

    vmem = pl.BlockSpec(memory_space=pltpu.VMEM)
    f32 = jnp.float32
    bf16 = jnp.bfloat16
    block, rows, spots = pl.pallas_call(
        exchange,
        out_shape=(
            jax.ShapeDtypeStruct((PIV, PIV), f32),
            jax.ShapeDtypeStruct((share, PIV), f32),
            jax.ShapeDtypeStruct((8, PIV), f32),
        ),
        in_specs=[vmem] * 3,
        out_specs=(vmem,) * 3,
        scratch_shapes=[
            pltpu.VMEM((X - 1, PIV // X, depth), bf16),
            pltpu.VMEM((PIV // X, depth), bf16),
            pltpu.VMEM((Z - 1, PIV // X, depth // Z), bf16),
            pltpu.VMEM((PIV // X, depth), bf16),
            pltpu.VMEM((PIV, depth), bf16),
            pltpu.VMEM((X - 1, 8, PIV), f32),
            pltpu.VMEM((Z - 1, 8, PIV), f32),
            pltpu.VMEM((V - 1, 8, PIV), f32),
            pltpu.VMEM((row_block, PIV), f32),
            pltpu.VMEM((PIV, PIV), f32),
            pltpu.VMEM((V - 1, share, PIV), f32),
            pltpu.VMEM((V - 1, PIV // V, PIV), f32),
            pltpu.SemaphoreType.DMA((3, X - 1)),
            pltpu.SemaphoreType.DMA((3, X - 1)),
            pltpu.SemaphoreType.DMA((3, Z - 1)),
            pltpu.SemaphoreType.DMA((3, Z - 1)),
            pltpu.SemaphoreType.DMA((4, V - 1)),
            pltpu.SemaphoreType.DMA((4, V - 1)),
        ],
        compiler_params=pltpu.CompilerParams(collective_id=0, has_side_effects=True),
    )(masked, old_vectors, spots)

    return pl.pallas_call(
        finish,
        out_shape=jax.ShapeDtypeStruct((share, PIV), f32),
        in_specs=[vmem] * 5,
        out_specs=vmem,
        scratch_shapes=[pltpu.VMEM((PIV + share, PIV), f32)],
    )(block, rows, spots, coords, (wanted - share_first)[None, :])


def solution(mesh):
    in_specs = (P(None, ("rows", "vecs")), P("rows", "vecs"), P(), P())
    out_specs = P(("rows", "vecs"), None)
    return jax.shard_map(shards, mesh=mesh, in_specs=in_specs, out_specs=out_specs, check_vma=False)
```
